32 devices in a mesh: frame: 2 (over x), tile: 16 (over z, y, core).
Axes of the slice: x: 2, y: 2, z: 4, core: 2. Of those that a mesh axis runs over, the one named last changes fastest.
Arguments:
- latents: bfloat16 [4, 64, 128, 512], P('frame', 'tile'), may hold values from -6 to 6
- conv_weight: bfloat16 [3, 3, 512, 512], replicated, may hold values from -0.09375 to 0.09375
- conv_bias: float32 [512], replicated, may hold values from -3 to 3
- query_weight: bfloat16 [512, 512], replicated, may hold values from -0.176776695 to 0.176776695
- key_weight: bfloat16 [512, 512], replicated, may hold values from -8 to 8
- value_weight: bfloat16 [512, 512], replicated, may hold values from -0.25 to 0.25
- out_weight: bfloat16 [512, 512], replicated, may hold values from -0.25 to 0.25
- cotangent: bfloat16 [4, 64, 128, 512], P('frame', 'tile'), may hold values from -0.032958984 to 0.032958984
Outputs:
- mixed_frames: bfloat16 [4, 64, 128, 512], P('frame', 'tile')
- conv_grad: float32 [512, 4608], P('tile', 'frame')
The draws below stay inside these ranges and needn't reach their ends.
All inputs are finite; a program needn't handle non-finite values.
Results may differ from the reference program's by a relative error of at most 0.0065.
Values may be sent and summed in bfloat16 or wider, within the bound.
A program may use at most 128 MiB of HBM per device.

```python
import math
import jax
import jax.numpy as jnp
from jax import lax

C = 512
HEADS = 8
COLS = 128
FRAMES = 4
HEIGHT = 64


def shared_pair(key):
    base = jnp.clip(jax.random.normal(jax.random.fold_in(key, 11), (C, C), jnp.float32), -4.0, 4.0) / math.sqrt(C)
    other = jnp.clip(jax.random.normal(jax.random.fold_in(key, 12), (C, C), jnp.float32), -4.0, 4.0) / math.sqrt(C)
    return (base, other)


def draw_query_weight(key, part):
    base, other = shared_pair(key)
    return base.astype(jnp.bfloat16)


def draw_key_weight(key, part):
    base, other = shared_pair(key)
    result = other
    return result.astype(jnp.bfloat16)


def spiked(array, rng, source, target, blocks, factor):
    def block_of(position):
        return (jnp.arange(array.shape[position]) // (array.shape[position] // blocks)).reshape((-1,) + (1,) * (array.ndim - 1 - position))

    one_side = jax.random.permutation(rng, blocks)[block_of(target)]
    far = (block_of(target) + blocks // 2) % blocks
    return jnp.where((block_of(source) == one_side) | (block_of(source) == far), factor * array, array)


def level_of(rng, extent, shards, least, largest):
    def one(dim, shards_of):
        heights = jax.random.uniform(jax.random.fold_in(jax.random.fold_in(rng, 6), dim), (shards_of,), jnp.float32, least / len(shards), largest / len(shards))
        return jnp.repeat(jnp.exp(heights), extent[dim] // shards_of).reshape((-1,) + (1,) * (len(extent) - dim - 1))

    loudness = one(*shards[0])
    for cut in shards[1:]:
        loudness = loudness * one(*cut)
    return loudness


def centred(stream_key, extent, spread, most, shards=(), dtype=jnp.bfloat16):
    gain = level_of(stream_key, extent, shards, -0.22, 0.18) if shards else 1.0
    drawn = jax.random.normal(stream_key, extent, jnp.float32) * spread * gain
    return jnp.minimum(jnp.maximum(drawn, -most), most).astype(dtype)


def gaussian_with(key, extent, spread, reach, cuts, heavy, kind=jnp.bfloat16):
    drawn = spread * jax.random.normal(key, extent, jnp.float32)
    if cuts:
        drawn = drawn * level_of(key, extent, cuts, -0.22, 0.18)
    return jnp.clip(spiked(drawn, jax.random.fold_in(key, 3), *heavy), -reach, reach).astype(kind)


def setup_inputs(seed: int = 0) -> dict:
    key_list = jax.random.split(jax.random.key(seed), 9)
    latents = centred(key_list[0], (FRAMES, HEIGHT, COLS, C), 1.0, 6.0, ((0, 2), (1, 16)))
    conv_weight = centred(key_list[1], (3, 3, C, C), (9 * C) ** -0.5, 0.09375)
    conv_bias = centred(key_list[2], (C,), 0.5, 3.0, (), jnp.float32)
    query_weight = draw_query_weight(jax.random.fold_in(key_list[8], 71), 0)
    key_weight = draw_key_weight(jax.random.fold_in(key_list[8], 71), 0)
    value_weight = centred(key_list[5], (C, C), C ** -0.5, 0.25)
    out_weight = centred(key_list[6], (C, C), C ** -0.5, 0.25)
    cotangent = gaussian_with(key_list[7], (FRAMES, HEIGHT, COLS, C), ((FRAMES * HEIGHT * COLS) ** -0.5), 0.032958984, ((0, 2), (1, 16)), (1, 3, 16, 2.0))
    return dict(latents=latents, conv_weight=conv_weight, conv_bias=conv_bias, query_weight=query_weight, key_weight=key_weight, value_weight=value_weight, out_weight=out_weight, cotangent=cotangent)


def attention(hidden, query_weight, key_weight, value_weight, out_weight):
    frames, height, cols, channels = hidden.shape
    head_dim = channels // HEADS
    tokens = hidden.astype(jnp.float32).reshape(-1, channels)
    queries = jnp.dot(tokens, query_weight.astype(jnp.float32), precision=lax.Precision.HIGHEST).astype(jnp.bfloat16)
    key_rows = jnp.dot(tokens, key_weight.astype(jnp.float32), precision=lax.Precision.HIGHEST).astype(jnp.bfloat16)
    values = jnp.dot(tokens, value_weight.astype(jnp.float32), precision=lax.Precision.HIGHEST).astype(jnp.bfloat16)
    shaped = (frames, height * cols, HEADS, head_dim)
    queries = queries.astype(jnp.float32).reshape(shaped)
    key_rows = key_rows.astype(jnp.float32).reshape(shaped)
    values = values.astype(jnp.float32).reshape(shaped)
    scores = jnp.einsum('fphd,gphd->phfg', queries, key_rows, precision=lax.Precision.HIGHEST) / math.sqrt(head_dim)
    weights = jax.nn.softmax(scores, axis=-1).astype(jnp.bfloat16).astype(jnp.float32)
    head_out = jnp.einsum('phfg,gphd->fphd', weights, values, precision=lax.Precision.HIGHEST).astype(jnp.bfloat16)
    projected = jnp.dot(head_out.astype(jnp.float32).reshape(-1, channels), out_weight.astype(jnp.float32), precision=lax.Precision.HIGHEST)
    mixed = tokens + projected
    return mixed.astype(jnp.bfloat16).reshape(frames, height, cols, channels)

def reference(latents, conv_weight, conv_bias, query_weight, key_weight, value_weight, out_weight, cotangent):
    convolved = lax.conv_general_dilated(latents.astype(jnp.float32), conv_weight.astype(jnp.float32), (1, 1), ((1, 1), (1, 1)), dimension_numbers=('NHWC', 'HWIO', 'NHWC'), precision=lax.Precision.HIGHEST)
    hidden = jax.nn.silu(convolved + conv_bias).astype(jnp.bfloat16)
    mixed_frames = attention(hidden, query_weight, key_weight, value_weight, out_weight)
    frames, height, cols, channels = mixed_frames.shape
    padded = jnp.pad(mixed_frames.astype(jnp.float32), ((0, 0), (1, 1), (1, 1), (0, 0)))
    flat_cot = cotangent.astype(jnp.float32).reshape(-1, channels)
    pieces = []
    for row_shift in range(3):
        for col_shift in range(3):
            shifted = padded[:, row_shift:row_shift + height, col_shift:col_shift + cols, :].reshape(-1, channels)
            pieces.append(lax.dot_general(flat_cot, shifted, (((0,), (0,)), ((), ())), precision=lax.Precision.HIGHEST))
    conv_grad = jnp.concatenate(pieces, axis=1)
    return (mixed_frames, conv_grad)
```

```python
import functools
import math

import jax
import jax.numpy as jnp
from jax import lax
from jax.experimental import pallas as pl
from jax.experimental.pallas import tpu as pltpu
from jax.sharding import PartitionSpec as P

HEADS = 8
LANES = 128
MESH = pl.DeviceIdType.MESH
F32 = jnp.float32
BF16 = jnp.bfloat16


def with_halo(cells, axis, dim):
    count = lax.axis_size(axis)
    ends = count - 1
    head = lax.slice_in_dim(cells, 0, 1, axis=dim)
    tail = lax.slice_in_dim(cells, cells.shape[dim] - 1, cells.shape[dim], axis=dim)
    return jnp.concatenate(
        [
            lax.ppermute(tail, axis, [(i, i + 1) for i in range(ends)]),
            cells,
            lax.ppermute(head, axis, [(i + 1, i) for i in range(ends)]),
        ],
        axis=dim,
    )


def attend_kernel(groups, own_ref, *refs):
    others = refs[: groups - 1]
    wq, wk, wv, wo, mixed_ref = refs[groups - 1 :]
    frames, pixels, channels = own_ref.shape
    head_dim = channels // HEADS
    own = own_ref[...].reshape(frames * pixels, channels)
    queries = jnp.dot(own, wq[...], preferred_element_type=F32).astype(BF16).astype(F32)
    keys, values = [], []
    for ref in (own_ref, *others):
        tokens = ref[...].reshape(frames * pixels, channels)
        k = jnp.dot(tokens, wk[...], preferred_element_type=F32).astype(BF16).astype(F32)
        v = jnp.dot(tokens, wv[...], preferred_element_type=F32).astype(BF16).astype(F32)
        for f in range(frames):
            keys.append(k[f * pixels : (f + 1) * pixels])
            values.append(v[f * pixels : (f + 1) * pixels])
    gather = (
        lax.broadcasted_iota(jnp.int32, (channels, LANES), 0) // head_dim
        == lax.broadcasted_iota(jnp.int32, (channels, LANES), 1)
    ).astype(F32).astype(BF16)
    spread = (
        lax.broadcasted_iota(jnp.int32, (LANES, channels), 1) // head_dim
        == lax.broadcasted_iota(jnp.int32, (LANES, channels), 0)
    ).astype(F32).astype(BF16)
    heads_out = []
    for f in range(frames):
        q = queries[f * pixels : (f + 1) * pixels]
        scores = []
        for k in keys:
            product = q * k
            high = product.astype(BF16)
            low = (product - high.astype(F32)).astype(BF16)
            total = jnp.dot(high, gather, preferred_element_type=F32) + jnp.dot(
                low, gather, preferred_element_type=F32
            )
            scores.append(total / math.sqrt(head_dim))
        top = functools.reduce(jnp.maximum, scores)
        exps = [jnp.exp(s - top) for s in scores]
        denom = functools.reduce(jnp.add, exps)
        acc = None
        for e, v in zip(exps, values):
            weight = (e / denom).astype(BF16)
            term = jnp.dot(weight, spread, preferred_element_type=F32) * v
            acc = term if acc is None else acc + term
        heads_out.append(acc.astype(BF16))
    projected = jnp.dot(jnp.concatenate(heads_out, axis=0), wo[...], preferred_element_type=F32)
    mixed = own.astype(F32) + projected
    mixed_ref[...] = mixed.astype(BF16).reshape(frames, pixels, channels)


def attend(parts, wq, wk, wv, wo):
    frames, pixels, channels = parts[0].shape
    block = min(LANES, pixels)
    token_spec = pl.BlockSpec((frames, block, channels), lambda i: (0, i, 0))
    weight_spec = pl.BlockSpec((channels, channels), lambda i: (0, 0))
    return pl.pallas_call(
        functools.partial(attend_kernel, len(parts)),
        grid=(pixels // block,),
        out_shape=jax.ShapeDtypeStruct(parts[0].shape, BF16),
        in_specs=[token_spec] * len(parts) + [weight_spec] * 4,
        out_specs=token_spec,
    )(*parts, wq, wk, wv, wo)


def bit_count(size):
    return size.bit_length() - 1


def grad_kernel(
    frames_n, tiles_n, taps_side, cols, cot_ref, mixed_ref, out_ref, part, recv, send_sem, recv_sem
):
    _, frames, out_channels, _ = cot_ref.shape
    channels = mixed_ref.shape[2]
    pixels = mixed_ref.shape[1]
    chunks, blocks, block_rows, width = part.shape
    fb, tb = bit_count(frames_n), bit_count(tiles_n)
    tile_bits = [("tile", b) for b in range(tb)]
    frame_bits = [("frame", b) for b in range(fb)]
    first, second, rest = tile_bits[:1], tile_bits[1:2], tile_bits[:1:-1]
    orders = (first + second + frame_bits + rest, first + frame_bits + second + rest)
    here = {"tile": lax.axis_index("tile"), "frame": lax.axis_index("frame")}

    def my_bit(axis, b):
        return lax.rem(here[axis] // (1 << b), 2)

    def partner(axis, b):
        return {axis: here[axis] + (1 - 2 * my_bit(axis, b)) * (1 << b)}

    stages = fb + tb
    barrier = pltpu.get_barrier_semaphore()
    for axis, b in orders[0]:
        pl.semaphore_signal(barrier, inc=1, device_id=partner(axis, b), device_id_type=MESH)
    pl.semaphore_wait(barrier, stages)

    def order_of(k):
        return orders[k % 2]

    def start_of(k, stage):
        total = 0
        for j in range(stage):
            total = total + my_bit(*order_of(k)[j]) * (blocks >> (j + 1))
        return total

    def copy_of(k, stage):
        axis, b = order_of(k)[stage]
        size = blocks >> (stage + 1)
        source = start_of(k, stage) + (1 - my_bit(axis, b)) * size
        return pltpu.make_async_remote_copy(
            src_ref=part.at[k, pl.ds(source, size)],
            dst_ref=recv.at[k, pl.ds(size, size)],
            send_sem=send_sem.at[k, stage],
            recv_sem=recv_sem.at[k, stage],
            device_id=partner(axis, b),
            device_id_type=MESH,
        )

    def compute(k):
        for f in range(frames_n):
            unit = f * chunks + k
            tap, col = (unit * width) // channels, (unit * width) % channels
            row_shift, col_shift = tap // taps_side, tap % taps_side
            lo = (taps_side - 1 - row_shift) * cols
            acc = None
            for g in range(frames):
                term = jnp.dot(
                    cot_ref[col_shift, g, :, lo : lo + pixels],
                    mixed_ref[g, :, col : col + width],
                    preferred_element_type=F32,
                )
                acc = term if acc is None else acc + term
            acc = acc.astype(BF16)
            for t in range(tiles_n):
                at = {"tile": t, "frame": f}
                place = 0
                for j, (axis, b) in enumerate(order_of(k)):
                    place += ((at[axis] >> b) & 1) * (blocks >> (j + 1))
                part[k, place] = acc[t * block_rows : (t + 1) * block_rows]

    def merge(k, stage):
        copy_of(k, stage).wait_recv()
        size = blocks >> (stage + 1)
        mine = start_of(k, stage + 1)
        got = recv[k, size : 2 * size].astype(F32)
        total = part[k, pl.ds(mine, size)].astype(F32) + got
        if stage < stages - 1:
            part[k, pl.ds(mine, size)] = total.astype(BF16)
            copy_of(k, stage + 1).start()
        else:
            out_ref[:, k * width : (k + 1) * width] = total[0]

    for step in range(chunks + stages):
        for stage in range(stages - 1, -1, -1):
            k = step - 1 - stage
            if 0 <= k < chunks:
                merge(k, stage)
        if step < chunks:
            compute(step)
            copy_of(step, 0).start()
    for k in range(chunks):
        for stage in range(stages):
            copy_of(k, stage).wait_send()


def kernel_grad(shifted_cot, mixed, cols):
    frames_n, tiles_n = lax.axis_size("frame"), lax.axis_size("tile")
    taps_side = shifted_cot.shape[0]
    out_channels, channels = shifted_cot.shape[2], mixed.shape[2]
    chunks = taps_side * taps_side
    width = channels // frames_n
    blocks, block_rows = frames_n * tiles_n, out_channels // tiles_n
    stages = bit_count(blocks)
    return pl.pallas_call(
        functools.partial(grad_kernel, frames_n, tiles_n, taps_side, cols),
        out_shape=jax.ShapeDtypeStruct((block_rows, chunks * width), F32),
        in_specs=[pl.BlockSpec(memory_space=pltpu.VMEM)] * 2,
        out_specs=pl.BlockSpec(memory_space=pltpu.VMEM),
        scratch_shapes=[
            pltpu.VMEM((chunks, blocks, block_rows, width), BF16),
            pltpu.VMEM((chunks, blocks, block_rows, width), BF16),
            pltpu.SemaphoreType.DMA((chunks, stages)),
            pltpu.SemaphoreType.DMA((chunks, stages)),
        ],
        compiler_params=pltpu.CompilerParams(
            collective_id=0, has_side_effects=True, vmem_limit_bytes=48 * 1024 * 1024
        ),
    )(shifted_cot, mixed)


def on_device(
    latents, conv_weight, conv_bias, query_weight, key_weight, value_weight, out_weight, cotangent
):
    frames, rows, cols, channels = latents.shape
    count = lax.axis_size("frame")
    padded = with_halo(latents, "tile", 1)
    convolved = lax.conv_general_dilated(
        padded,
        conv_weight,
        (1, 1),
        ((0, 0), (1, 1)),
        dimension_numbers=("NHWC", "HWIO", "NHWC"),
        preferred_element_type=F32,
    )
    hidden = jax.nn.silu(convolved + conv_bias).astype(BF16).reshape(frames, rows * cols, channels)
    parts = [hidden] + [
        lax.ppermute(hidden, "frame", [(i, (i + k) % count) for i in range(count)])
        for k in range(1, count)
    ]
    mixed = attend(parts, query_weight, key_weight, value_weight, out_weight)
    turned = with_halo(cotangent, "tile", 1).transpose(0, 3, 1, 2)
    side = conv_weight.shape[1]
    wide = jnp.pad(turned, ((0, 0), (0, 0), (0, 0), (1, 1)))
    shifted_cot = jnp.stack(
        [wide[..., side - 1 - s : side - 1 - s + cols] for s in range(side)]
    ).reshape(side, frames, channels, (rows + 2) * cols)
    conv_grad = kernel_grad(shifted_cot, mixed, cols)
    return (mixed.reshape(frames, rows, cols, channels), conv_grad)


def solution(mesh):
    in_specs = (
        P("frame", "tile", None, None),
        P(),
        P(),
        P(),
        P(),
        P(),
        P(),
        P("frame", "tile", None, None),
    )
    out_specs = (P("frame", "tile", None, None), P("tile", "frame"))
    return jax.shard_map(
        on_device, mesh=mesh, in_specs=in_specs, out_specs=out_specs, check_vma=False
    )
```

```python
import functools
import math

import jax
import jax.numpy as jnp
from jax import lax
from jax.experimental import pallas as pl
from jax.experimental.pallas import tpu as pltpu
from jax.sharding import PartitionSpec as P

HEADS = 8
LANES = 128
MESH = pl.DeviceIdType.MESH
F32 = jnp.float32
BF16 = jnp.bfloat16


def with_halo(cells, axis, dim):
    count = lax.axis_size(axis)
    ends = count - 1
    head = lax.slice_in_dim(cells, 0, 1, axis=dim)
    tail = lax.slice_in_dim(cells, cells.shape[dim] - 1, cells.shape[dim], axis=dim)
    return jnp.concatenate(
        [
            lax.ppermute(tail, axis, [(i, i + 1) for i in range(ends)]),
            cells,
            lax.ppermute(head, axis, [(i + 1, i) for i in range(ends)]),
        ],
        axis=dim,
    )


def attend_kernel(groups, own_ref, *refs):
    others = refs[: groups - 1]
    wq, wk, wv, wo, mixed_ref = refs[groups - 1 :]
    frames, pixels, channels = own_ref.shape
    head_dim = channels // HEADS
    own = own_ref[...].reshape(frames * pixels, channels)
    queries = jnp.dot(own, wq[...], preferred_element_type=F32).astype(BF16).astype(F32)
    keys, values = [], []
    for ref in (own_ref, *others):
        tokens = ref[...].reshape(frames * pixels, channels)
        k = jnp.dot(tokens, wk[...], preferred_element_type=F32).astype(BF16).astype(F32)
        v = jnp.dot(tokens, wv[...], preferred_element_type=F32).astype(BF16).astype(F32)
        for f in range(frames):
            keys.append(k[f * pixels : (f + 1) * pixels])
            values.append(v[f * pixels : (f + 1) * pixels])
    gather = (
        lax.broadcasted_iota(jnp.int32, (channels, LANES), 0) // head_dim
        == lax.broadcasted_iota(jnp.int32, (channels, LANES), 1)
    ).astype(F32).astype(BF16)
    spread = (
        lax.broadcasted_iota(jnp.int32, (LANES, channels), 1) // head_dim
        == lax.broadcasted_iota(jnp.int32, (LANES, channels), 0)
    ).astype(F32).astype(BF16)
    heads_out = []
    for f in range(frames):
        q = queries[f * pixels : (f + 1) * pixels]
        scores = []
        for k in keys:
            product = q * k
            high = product.astype(BF16)
            low = (product - high.astype(F32)).astype(BF16)
            total = jnp.dot(high, gather, preferred_element_type=F32) + jnp.dot(
                low, gather, preferred_element_type=F32
            )
            scores.append(total / math.sqrt(head_dim))
        top = functools.reduce(jnp.maximum, scores)
        exps = [jnp.exp(s - top) for s in scores]
        denom = functools.reduce(jnp.add, exps)
        acc = None
        for e, v in zip(exps, values):
            weight = (e / denom).astype(BF16)
            term = jnp.dot(weight, spread, preferred_element_type=F32) * v
            acc = term if acc is None else acc + term
        heads_out.append(acc.astype(BF16))
    projected = jnp.dot(jnp.concatenate(heads_out, axis=0), wo[...], preferred_element_type=F32)
    mixed = own.astype(F32) + projected
    mixed_ref[...] = mixed.astype(BF16).reshape(frames, pixels, channels)


def attend(parts, wq, wk, wv, wo):
    frames, pixels, channels = parts[0].shape
    block = min(LANES, pixels)
    token_spec = pl.BlockSpec((frames, block, channels), lambda i: (0, i, 0))
    weight_spec = pl.BlockSpec((channels, channels), lambda i: (0, 0))
    return pl.pallas_call(
        functools.partial(attend_kernel, len(parts)),
        grid=(pixels // block,),
        out_shape=jax.ShapeDtypeStruct(parts[0].shape, BF16),
        in_specs=[token_spec] * len(parts) + [weight_spec] * 4,
        out_specs=token_spec,
    )(*parts, wq, wk, wv, wo)


def bit_count(size):
    return size.bit_length() - 1


def split_bits(frames_n, tiles_n):
    tile_bits = [("tile", b) for b in range(bit_count(tiles_n))]
    frame_bits = [("frame", b) for b in range(bit_count(frames_n))]
    first, second, rest = tile_bits[:1], tile_bits[1:2], tile_bits[2:]
    return (first + second + frame_bits, first + frame_bits + second), rest


def grad_kernel(
    frames_n, tiles_n, taps_side, cols, cot_ref, mixed_ref, out_ref, part, recv, send_sem, recv_sem
):
    _, frames, out_channels, _ = cot_ref.shape
    channels = mixed_ref.shape[2]
    pixels = mixed_ref.shape[1]
    chunks, blocks, block_rows, width = part.shape
    orders, rest = split_bits(frames_n, tiles_n)
    halvings = len(orders[0])
    group = 1 << len(rest)
    here = {"tile": lax.axis_index("tile"), "frame": lax.axis_index("frame")}

    def my_bit(axis, b):
        return lax.rem(here[axis] // (1 << b), 2)

    def partner(axis, b):
        return {axis: here[axis] + (1 - 2 * my_bit(axis, b)) * (1 << b)}

    def flipped(mask):
        tile, place = here["tile"], 0
        for j, (axis, b) in enumerate(rest):
            bit = my_bit(axis, b)
            turned = 1 - bit if (mask >> j) & 1 else bit
            tile = tile + (turned - bit) * (1 << b)
            place = place + turned * (1 << j)
        return {"tile": tile}, place

    barrier = pltpu.get_barrier_semaphore()
    friends = [partner(axis, b) for axis, b in orders[0]]
    friends += [flipped(mask)[0] for mask in range(1, group)]
    for friend in friends:
        pl.semaphore_signal(barrier, inc=1, device_id=friend, device_id_type=MESH)
    pl.semaphore_wait(barrier, len(friends))

    def order_of(k):
        return orders[k % 2]

    def start_of(k, stage):
        total = 0
        for j in range(stage):
            total = total + my_bit(*order_of(k)[j]) * (blocks >> (j + 1))
        return total

    def copies_of(k, stage):
        if stage < halvings:
            axis, b = order_of(k)[stage]
            size = blocks >> (stage + 1)
            source = start_of(k, stage) + (1 - my_bit(axis, b)) * size
            todo = [(source, size, size, stage, partner(axis, b))]
        else:
            base = start_of(k, halvings)
            todo = []
            for mask in range(1, group):
                device, place = flipped(mask)
                todo.append((base + place, 1, mask, halvings + mask - 1, device))
        return [
            pltpu.make_async_remote_copy(
                src_ref=part.at[k, pl.ds(source, size)],
                dst_ref=recv.at[k, pl.ds(target, size)],
                send_sem=send_sem.at[k, sem],
                recv_sem=recv_sem.at[k, sem],
                device_id=device,
                device_id_type=MESH,
            )
            for source, size, target, sem, device in todo
        ]

    def compute(k):
        for f in range(frames_n):
            unit = f * chunks + k
            tap, col = (unit * width) // channels, (unit * width) % channels
            row_shift, col_shift = tap // taps_side, tap % taps_side
            lo = (taps_side - 1 - row_shift) * cols
            acc = None
            for g in range(frames):
                term = jnp.dot(
                    cot_ref[col_shift, g, :, lo : lo + pixels],
                    mixed_ref[g, :, col : col + width],
                    preferred_element_type=F32,
                )
                acc = term if acc is None else acc + term
            acc = acc.astype(BF16)
            for t in range(tiles_n):
                at = {"tile": t, "frame": f}
                place = 0
                for j, (axis, b) in enumerate(order_of(k)):
                    place += ((at[axis] >> b) & 1) * (blocks >> (j + 1))
                for j, (axis, b) in enumerate(rest):
                    place += ((at[axis] >> b) & 1) << j
                part[k, place] = acc[t * block_rows : (t + 1) * block_rows]

    def merge(k, stage):
        for copy in copies_of(k, stage):
            copy.wait_recv()
        if stage < halvings:
            size = blocks >> (stage + 1)
            mine = start_of(k, stage + 1)
            got = recv[k, size : 2 * size].astype(F32)
            total = part[k, pl.ds(mine, size)].astype(F32) + got
            part[k, pl.ds(mine, size)] = total.astype(BF16)
            for copy in copies_of(k, stage + 1):
                copy.start()
        else:
            total = part[k, start_of(k, halvings) + flipped(0)[1]].astype(F32)
            for mask in range(1, group):
                total = total + recv[k, mask].astype(F32)
            out_ref[:, k * width : (k + 1) * width] = total

    due = [2, 5] + [7 + 2 * j for j in range(halvings - 2)] + [7 + 2 * (halvings - 2)]
    for step in range(chunks + due[halvings]):
        for stage in range(halvings, -1, -1):
            k = step - due[stage]
            if 0 <= k < chunks:
                merge(k, stage)
        if step < chunks:
            compute(step)
            for copy in copies_of(step, 0):
                copy.start()
    for k in range(chunks):
        for stage in range(halvings + 1):
            for copy in copies_of(k, stage):
                copy.wait_send()


def kernel_grad(shifted_cot, mixed, cols):
    frames_n, tiles_n = lax.axis_size("frame"), lax.axis_size("tile")
    taps_side = shifted_cot.shape[0]
    out_channels, channels = shifted_cot.shape[2], mixed.shape[2]
    chunks = taps_side * taps_side
    width = channels // frames_n
    blocks, block_rows = frames_n * tiles_n, out_channels // tiles_n
    orders, rest = split_bits(frames_n, tiles_n)
    stages = len(orders[0]) + (1 << len(rest)) - 1
    return pl.pallas_call(
        functools.partial(grad_kernel, frames_n, tiles_n, taps_side, cols),
        out_shape=jax.ShapeDtypeStruct((block_rows, chunks * width), F32),
        in_specs=[pl.BlockSpec(memory_space=pltpu.VMEM)] * 2,
        out_specs=pl.BlockSpec(memory_space=pltpu.VMEM),
        scratch_shapes=[
            pltpu.VMEM((chunks, blocks, block_rows, width), BF16),
            pltpu.VMEM((chunks, blocks, block_rows, width), BF16),
            pltpu.SemaphoreType.DMA((chunks, stages)),
            pltpu.SemaphoreType.DMA((chunks, stages)),
        ],
        compiler_params=pltpu.CompilerParams(
            collective_id=0, has_side_effects=True, vmem_limit_bytes=48 * 1024 * 1024
        ),
    )(shifted_cot, mixed)


def on_device(
    latents, conv_weight, conv_bias, query_weight, key_weight, value_weight, out_weight, cotangent
):
    frames, rows, cols, channels = latents.shape
    count = lax.axis_size("frame")
    padded = with_halo(latents, "tile", 1)
    convolved = lax.conv_general_dilated(
        padded,
        conv_weight,
        (1, 1),
        ((0, 0), (1, 1)),
        dimension_numbers=("NHWC", "HWIO", "NHWC"),
        preferred_element_type=F32,
    )
    hidden = jax.nn.silu(convolved + conv_bias).astype(BF16).reshape(frames, rows * cols, channels)
    parts = [hidden] + [
        lax.ppermute(hidden, "frame", [(i, (i + k) % count) for i in range(count)])
        for k in range(1, count)
    ]
    mixed = attend(parts, query_weight, key_weight, value_weight, out_weight)
    turned = with_halo(cotangent, "tile", 1).transpose(0, 3, 1, 2)
    side = conv_weight.shape[1]
    wide = jnp.pad(turned, ((0, 0), (0, 0), (0, 0), (1, 1)))
    shifted_cot = jnp.stack(
        [wide[..., side - 1 - s : side - 1 - s + cols] for s in range(side)]
    ).reshape(side, frames, channels, (rows + 2) * cols)
    conv_grad = kernel_grad(shifted_cot, mixed, cols)
    return (mixed.reshape(frames, rows, cols, channels), conv_grad)


def solution(mesh):
    in_specs = (
        P("frame", "tile", None, None),
        P(),
        P(),
        P(),
        P(),
        P(),
        P(),
        P("frame", "tile", None, None),
    )
    out_specs = (P("frame", "tile", None, None), P("tile", "frame"))
    return jax.shard_map(
        on_device, mesh=mesh, in_specs=in_specs, out_specs=out_specs, check_vma=False
    )
```

```python
import functools
import math

import jax
import jax.numpy as jnp
from jax import lax
from jax.experimental import pallas as pl
from jax.experimental.pallas import tpu as pltpu
from jax.sharding import PartitionSpec as P

HEADS = 8
LANES = 128
MESH = pl.DeviceIdType.MESH
F32 = jnp.float32
BF16 = jnp.bfloat16


def attend(token_parts, wq, wk, wv, wo, frames):
    own = token_parts[0]
    channels = own.shape[1]
    pixels = own.shape[0] // frames
    head_dim = channels // HEADS
    queries = jnp.dot(own, wq[...], preferred_element_type=F32).astype(BF16).astype(F32)
    keys, values = [], []
    for tokens in token_parts:
        k = jnp.dot(tokens, wk[...], preferred_element_type=F32).astype(BF16).astype(F32)
        v = jnp.dot(tokens, wv[...], preferred_element_type=F32).astype(BF16).astype(F32)
        for f in range(frames):
            keys.append(k[f * pixels : (f + 1) * pixels])
            values.append(v[f * pixels : (f + 1) * pixels])
    gather = (
        lax.broadcasted_iota(jnp.int32, (channels, LANES), 0) // head_dim
        == lax.broadcasted_iota(jnp.int32, (channels, LANES), 1)
    ).astype(F32).astype(BF16)
    spread = (
        lax.broadcasted_iota(jnp.int32, (LANES, channels), 1) // head_dim
        == lax.broadcasted_iota(jnp.int32, (LANES, channels), 0)
    ).astype(F32).astype(BF16)
    heads_out = []
    for f in range(frames):
        q = queries[f * pixels : (f + 1) * pixels]
        scores = []
        for k in keys:
            product = q * k
            high = product.astype(BF16)
            low = (product - high.astype(F32)).astype(BF16)
            total = jnp.dot(high, gather, preferred_element_type=F32) + jnp.dot(
                low, gather, preferred_element_type=F32
            )
            scores.append(total / math.sqrt(head_dim))
        top = functools.reduce(jnp.maximum, scores)
        exps = [jnp.exp(s - top) for s in scores]
        denom = functools.reduce(jnp.add, exps)
        acc = None
        for e, v in zip(exps, values):
            weight = (e / denom).astype(BF16)
            term = jnp.dot(weight, spread, preferred_element_type=F32) * v
            acc = term if acc is None else acc + term
        heads_out.append(acc.astype(BF16))
    projected = jnp.dot(jnp.concatenate(heads_out, axis=0), wo[...], preferred_element_type=F32)
    mixed = own.astype(F32) + projected
    return mixed.astype(BF16)


def front_kernel(
    lat_ref, conv_ref, bias_ref, wq, wk, wv, wo, cot_ref,
    mixed_ref, turned_ref,
    lat_rim, cot_rim, moved, hidden, others,
    rim_send, rim_recv, hid_send, hid_recv,
):
    frames, rows, cols, channels = lat_ref.shape
    side = conv_ref.shape[0]
    count, tiles = lax.axis_size("frame"), lax.axis_size("tile")
    frame, tile = lax.axis_index("frame"), lax.axis_index("tile")
    has = (tile > 0, tile < tiles - 1)
    beside = (tile - 1, tile + 1)

    barrier = pltpu.get_barrier_semaphore()
    for step in (1, tiles - 1):
        pl.semaphore_signal(
            barrier, inc=1, device_id={"tile": lax.rem(tile + step, tiles)}, device_id_type=MESH
        )
    for k in range(1, count):
        pl.semaphore_signal(
            barrier, inc=1, device_id={"frame": lax.rem(frame + k, count)}, device_id_type=MESH
        )
    pl.semaphore_wait(barrier, 2 + count - 1)

    def rim_copy(which, end):
        source, target = ((lat_ref, lat_rim), (cot_ref, cot_rim))[which]
        return pltpu.make_async_remote_copy(
            src_ref=source.at[:, (rows - 1) * end],
            dst_ref=target.at[1 - end],
            send_sem=rim_send.at[which, end],
            recv_sem=rim_recv.at[which, 1 - end],
            device_id={"tile": beside[end]},
            device_id_type=MESH,
        )

    def rim_arrival(which, end):
        source, target = ((lat_ref, lat_rim), (cot_ref, cot_rim))[which]
        return pltpu.make_async_remote_copy(
            src_ref=source.at[:, (rows - 1) * end],
            dst_ref=target.at[end],
            send_sem=rim_send.at[which, end],
            recv_sem=rim_recv.at[which, end],
            device_id={"tile": beside[end]},
            device_id_type=MESH,
        )

    for which in range(2):
        for end in range(2):

            @pl.when(has[end])
            def _():
                rim_copy(which, end).start()

    def settle(which):
        target = (lat_rim, cot_rim)[which]
        for end in range(2):

            @pl.when(has[end])
            def _():
                rim_arrival(which, end).wait_recv()

            @pl.when(jnp.logical_not(has[end]))
            def _():
                target[end] = jnp.zeros_like(target[end])

    def by_column(value, offset):
        if offset == 0:
            return value
        wide = value.astype(F32)
        rolled = pltpu.roll(wide, (-offset) % cols, 0)
        at = lax.broadcasted_iota(jnp.int32, wide.shape, 0)
        edge = 0 if offset < 0 else cols - 1
        return jnp.where(at == edge, 0.0, rolled).astype(BF16)

    def place(value, f, row):
        for s in range(side):
            moved[s, f, row] = by_column(value, s - 1)

    def convolve(row):
        acc = jnp.broadcast_to(bias_ref[...], (frames * cols, channels))
        for r in range(side):
            for s in range(side):
                acc = acc + jnp.dot(
                    moved[s, :, row + r].reshape(frames * cols, channels),
                    conv_ref[r, s],
                    preferred_element_type=F32,
                )
        result = acc / (1.0 + jnp.exp(-acc))
        hidden[row] = result.astype(BF16)
        for k in range(1, count):
            hidden_copy(k, row).start()

    def hidden_copy(k, row):
        return pltpu.make_async_remote_copy(
            src_ref=hidden.at[row],
            dst_ref=others.at[k - 1, row],
            send_sem=hid_send.at[k - 1, row],
            recv_sem=hid_recv.at[k - 1, row],
            device_id={"frame": lax.rem(frame + k, count)},
            device_id_type=MESH,
        )

    for row in range(rows):
        for f in range(frames):
            place(lat_ref[f, row], f, row + 1)
    for row in range(1, rows - 1):
        convolve(row)
    settle(0)
    for f in range(frames):
        place(lat_rim[0, f], f, 0)
        place(lat_rim[1, f], f, rows + 1)
    for row in (rows - 1, 0):
        convolve(row)

    def turn(value, f, row):
        for s in range(side):
            turned_ref[s, f, :, row * cols : (row + 1) * cols] = by_column(value, 1 - s).T

    for row in range(rows):
        for f in range(frames):
            turn(cot_ref[f, row], f, row + 1)
    settle(1)
    for f in range(frames):
        turn(cot_rim[0, f], f, 0)
        turn(cot_rim[1, f], f, rows + 1)

    def attend_row(i, carry):
        row = lax.rem(i + 1, rows)
        for k in range(1, count):
            hidden_copy(k, row).wait_recv()
        parts = [hidden[row]] + [others[k - 1, row] for k in range(1, count)]
        mixed = attend(parts, wq, wk, wv, wo, frames)
        for f in range(frames):
            mixed_ref[f, pl.ds(pl.multiple_of(row * cols, cols), cols)] = mixed[
                f * cols : (f + 1) * cols
            ]
        return carry

    lax.fori_loop(0, rows, attend_row, 0)
    for row in range(rows):
        for k in range(1, count):
            hidden_copy(k, row).wait_send()
    for which in range(2):
        for end in range(2):

            @pl.when(has[end])
            def _():
                rim_copy(which, end).wait_send()


def front(latents, conv_weight, conv_bias, wq, wk, wv, wo, cotangent):
    frames, rows, cols, channels = latents.shape
    side = conv_weight.shape[0]
    count = lax.axis_size("frame")
    return pl.pallas_call(
        front_kernel,
        out_shape=[
            jax.ShapeDtypeStruct((frames, rows * cols, channels), BF16),
            jax.ShapeDtypeStruct((side, frames, channels, (rows + 2) * cols), BF16),
        ],
        in_specs=[pl.BlockSpec(memory_space=pltpu.VMEM)] * 8,
        out_specs=[pl.BlockSpec(memory_space=pltpu.VMEM)] * 2,
        scratch_shapes=[
            pltpu.VMEM((2, frames, cols, channels), BF16),
            pltpu.VMEM((2, frames, cols, channels), BF16),
            pltpu.VMEM((side, frames, rows + 2, cols, channels), BF16),
            pltpu.VMEM((rows, frames * cols, channels), BF16),
            pltpu.VMEM((count - 1, rows, frames * cols, channels), BF16),
            pltpu.SemaphoreType.DMA((2, 2)),
            pltpu.SemaphoreType.DMA((2, 2)),
            pltpu.SemaphoreType.DMA((count - 1, rows)),
            pltpu.SemaphoreType.DMA((count - 1, rows)),
        ],
        compiler_params=pltpu.CompilerParams(
            collective_id=1, has_side_effects=True, vmem_limit_bytes=56 * 1024 * 1024
        ),
    )(latents, conv_weight, conv_bias.reshape(1, -1), wq, wk, wv, wo, cotangent)


def bit_count(size):
    return size.bit_length() - 1


def split_bits(frames_n, tiles_n):
    tile_bits = [("tile", b) for b in range(bit_count(tiles_n))]
    frame_bits = [("frame", b) for b in range(bit_count(frames_n))]
    first, second, rest = tile_bits[:1], tile_bits[1:2], tile_bits[2:]
    return (first + second + frame_bits, first + frame_bits + second), rest


def grad_kernel(
    frames_n, tiles_n, taps_side, cols, cot_ref, mixed_ref, out_ref, part, recv, send_sem, recv_sem
):
    _, frames, out_channels, _ = cot_ref.shape
    channels = mixed_ref.shape[2]
    pixels = mixed_ref.shape[1]
    chunks, blocks, block_rows, width = part.shape
    orders, rest = split_bits(frames_n, tiles_n)
    halvings = len(orders[0])
    group = 1 << len(rest)
    here = {"tile": lax.axis_index("tile"), "frame": lax.axis_index("frame")}

    def my_bit(axis, b):
        return lax.rem(here[axis] // (1 << b), 2)

    def partner(axis, b):
        return {axis: here[axis] + (1 - 2 * my_bit(axis, b)) * (1 << b)}

    def flipped(mask):
        tile, place = here["tile"], 0
        for j, (axis, b) in enumerate(rest):
            bit = my_bit(axis, b)
            turned = 1 - bit if (mask >> j) & 1 else bit
            tile = tile + (turned - bit) * (1 << b)
            place = place + turned * (1 << j)
        return {"tile": tile}, place

    barrier = pltpu.get_barrier_semaphore()
    friends = [partner(axis, b) for axis, b in orders[0]]
    friends += [flipped(mask)[0] for mask in range(1, group)]
    for friend in friends:
        pl.semaphore_signal(barrier, inc=1, device_id=friend, device_id_type=MESH)
    pl.semaphore_wait(barrier, len(friends))

    def order_of(k):
        return orders[k % 2]

    def start_of(k, stage):
        total = 0
        for j in range(stage):
            total = total + my_bit(*order_of(k)[j]) * (blocks >> (j + 1))
        return total

    def copies_of(k, stage):
        if stage < halvings:
            axis, b = order_of(k)[stage]
            size = blocks >> (stage + 1)
            source = start_of(k, stage) + (1 - my_bit(axis, b)) * size
            todo = [(source, size, size, stage, partner(axis, b))]
        else:
            base = start_of(k, halvings)
            todo = []
            for mask in range(1, group):
                device, place = flipped(mask)
                todo.append((base + place, 1, mask, halvings + mask - 1, device))
        return [
            pltpu.make_async_remote_copy(
                src_ref=part.at[k, pl.ds(source, size)],
                dst_ref=recv.at[k, pl.ds(target, size)],
                send_sem=send_sem.at[k, sem],
                recv_sem=recv_sem.at[k, sem],
                device_id=device,
                device_id_type=MESH,
            )
            for source, size, target, sem, device in todo
        ]

    def compute(k):
        for f in range(frames_n):
            unit = f * chunks + k
            tap, col = (unit * width) // channels, (unit * width) % channels
            row_shift, col_shift = tap // taps_side, tap % taps_side
            lo = (taps_side - 1 - row_shift) * cols
            acc = None
            for g in range(frames):
                term = jnp.dot(
                    cot_ref[col_shift, g, :, lo : lo + pixels],
                    mixed_ref[g, :, col : col + width],
                    preferred_element_type=F32,
                )
                acc = term if acc is None else acc + term
            acc = acc.astype(BF16)
            for t in range(tiles_n):
                at = {"tile": t, "frame": f}
                place = 0
                for j, (axis, b) in enumerate(order_of(k)):
                    place += ((at[axis] >> b) & 1) * (blocks >> (j + 1))
                for j, (axis, b) in enumerate(rest):
                    place += ((at[axis] >> b) & 1) << j
                part[k, place] = acc[t * block_rows : (t + 1) * block_rows]

    def merge(k, stage):
        for copy in copies_of(k, stage):
            copy.wait_recv()
        if stage < halvings:
            size = blocks >> (stage + 1)
            mine = start_of(k, stage + 1)
            got = recv[k, size : 2 * size].astype(F32)
            total = part[k, pl.ds(mine, size)].astype(F32) + got
            part[k, pl.ds(mine, size)] = total.astype(BF16)
            for copy in copies_of(k, stage + 1):
                copy.start()
        else:
            total = part[k, start_of(k, halvings) + flipped(0)[1]].astype(F32)
            for mask in range(1, group):
                total = total + recv[k, mask].astype(F32)
            out_ref[:, k * width : (k + 1) * width] = total

    due = [2, 5] + [7 + 2 * j for j in range(halvings - 2)] + [7 + 2 * (halvings - 2)]
    for step in range(chunks + due[halvings]):
        for stage in range(halvings, -1, -1):
            k = step - due[stage]
            if 0 <= k < chunks:
                merge(k, stage)
        if step < chunks:
            compute(step)
            for copy in copies_of(step, 0):
                copy.start()
    for k in range(chunks):
        for stage in range(halvings + 1):
            for copy in copies_of(k, stage):
                copy.wait_send()


def kernel_grad(shifted_cot, mixed, cols):
    frames_n, tiles_n = lax.axis_size("frame"), lax.axis_size("tile")
    taps_side = shifted_cot.shape[0]
    out_channels, channels = shifted_cot.shape[2], mixed.shape[2]
    chunks = taps_side * taps_side
    width = channels // frames_n
    blocks, block_rows = frames_n * tiles_n, out_channels // tiles_n
    orders, rest = split_bits(frames_n, tiles_n)
    stages = len(orders[0]) + (1 << len(rest)) - 1
    return pl.pallas_call(
        functools.partial(grad_kernel, frames_n, tiles_n, taps_side, cols),
        out_shape=jax.ShapeDtypeStruct((block_rows, chunks * width), F32),
        in_specs=[pl.BlockSpec(memory_space=pltpu.VMEM)] * 2,
        out_specs=pl.BlockSpec(memory_space=pltpu.VMEM),
        scratch_shapes=[
            pltpu.VMEM((chunks, blocks, block_rows, width), BF16),
            pltpu.VMEM((chunks, blocks, block_rows, width), BF16),
            pltpu.SemaphoreType.DMA((chunks, stages)),
            pltpu.SemaphoreType.DMA((chunks, stages)),
        ],
        compiler_params=pltpu.CompilerParams(
            collective_id=0, has_side_effects=True, vmem_limit_bytes=48 * 1024 * 1024
        ),
    )(shifted_cot, mixed)


def on_device(
    latents, conv_weight, conv_bias, query_weight, key_weight, value_weight, out_weight, cotangent
):
    frames, rows, cols, channels = latents.shape
    mixed, shifted_cot = front(
        latents, conv_weight, conv_bias, query_weight, key_weight, value_weight, out_weight, cotangent
    )
    conv_grad = kernel_grad(shifted_cot, mixed, cols)
    return (mixed.reshape(frames, rows, cols, channels), conv_grad)


def solution(mesh):
    in_specs = (
        P("frame", "tile", None, None),
        P(),
        P(),
        P(),
        P(),
        P(),
        P(),
        P("frame", "tile", None, None),
    )
    out_specs = (P("frame", "tile", None, None), P("tile", "frame"))
    return jax.shard_map(
        on_device, mesh=mesh, in_specs=in_specs, out_specs=out_specs, check_vma=False
    )
```

```python
import functools
import math
from types import SimpleNamespace

import jax
import jax.numpy as jnp
from jax import lax
from jax.experimental import pallas as pl
from jax.experimental.pallas import tpu as pltpu
from jax.sharding import PartitionSpec as P

HEADS = 8
LANES = 128
MESH = pl.DeviceIdType.MESH
F32 = jnp.float32
BF16 = jnp.bfloat16


def attend(token_parts, wq, wk, wv, wo, frames):
    own = token_parts[0]
    channels = own.shape[1]
    pixels = own.shape[0] // frames
    head_dim = channels // HEADS
    queries = jnp.dot(own, wq[...], preferred_element_type=F32).astype(BF16).astype(F32)
    keys, values = [], []
    for tokens in token_parts:
        k = jnp.dot(tokens, wk[...], preferred_element_type=F32).astype(BF16).astype(F32)
        v = jnp.dot(tokens, wv[...], preferred_element_type=F32).astype(BF16).astype(F32)
        for f in range(frames):
            keys.append(k[f * pixels : (f + 1) * pixels])
            values.append(v[f * pixels : (f + 1) * pixels])
    gather = (
        lax.broadcasted_iota(jnp.int32, (channels, LANES), 0) // head_dim
        == lax.broadcasted_iota(jnp.int32, (channels, LANES), 1)
    ).astype(F32).astype(BF16)
    spread = (
        lax.broadcasted_iota(jnp.int32, (LANES, channels), 1) // head_dim
        == lax.broadcasted_iota(jnp.int32, (LANES, channels), 0)
    ).astype(F32).astype(BF16)
    heads_out = []
    for f in range(frames):
        q = queries[f * pixels : (f + 1) * pixels]
        scores = []
        for k in keys:
            product = q * k
            high = product.astype(BF16)
            low = (product - high.astype(F32)).astype(BF16)
            total = jnp.dot(high, gather, preferred_element_type=F32) + jnp.dot(
                low, gather, preferred_element_type=F32
            )
            scores.append(total / math.sqrt(head_dim))
        top = functools.reduce(jnp.maximum, scores)
        exps = [jnp.exp(s - top) for s in scores]
        denom = functools.reduce(jnp.add, exps)
        acc = None
        for e, v in zip(exps, values):
            weight = (e / denom).astype(BF16)
            term = jnp.dot(weight, spread, preferred_element_type=F32) * v
            acc = term if acc is None else acc + term
        heads_out.append(acc.astype(BF16))
    projected = jnp.dot(jnp.concatenate(heads_out, axis=0), wo[...], preferred_element_type=F32)
    mixed = own.astype(F32) + projected
    return mixed.astype(BF16)


def bit_count(size):
    return size.bit_length() - 1


def split_bits(frames_n, tiles_n):
    tile_bits = [("tile", b) for b in range(bit_count(tiles_n))]
    frame_bits = [("frame", b) for b in range(bit_count(frames_n))]
    first, second, rest = tile_bits[:1], tile_bits[1:2], tile_bits[2:]
    return (first + second + frame_bits, first + frame_bits + second), rest


def reduction_of(taps_side, cols, cot_ref, mixed_ref, out_ref, part, recv, send_sem, recv_sem):
    frames = cot_ref.shape[1]
    frames_n, tiles_n = lax.axis_size("frame"), lax.axis_size("tile")
    channels = mixed_ref.shape[2]
    pixels = mixed_ref.shape[1]
    chunks, blocks, block_rows, width = part.shape
    orders, rest = split_bits(frames_n, tiles_n)
    halvings = len(orders[0])
    group = 1 << len(rest)
    here = {"tile": lax.axis_index("tile"), "frame": lax.axis_index("frame")}

    def my_bit(axis, b):
        return lax.rem(here[axis] // (1 << b), 2)

    def partner(axis, b):
        return {axis: here[axis] + (1 - 2 * my_bit(axis, b)) * (1 << b)}

    def flipped(mask):
        tile, place = here["tile"], 0
        for j, (axis, b) in enumerate(rest):
            bit = my_bit(axis, b)
            turned = 1 - bit if (mask >> j) & 1 else bit
            tile = tile + (turned - bit) * (1 << b)
            place = place + turned * (1 << j)
        return {"tile": tile}, place

    friends = [partner(axis, b) for axis, b in orders[0]]
    friends += [flipped(mask)[0] for mask in range(1, group)]
    def order_of(k):
        return orders[k % 2]

    def start_of(k, stage):
        total = 0
        for j in range(stage):
            total = total + my_bit(*order_of(k)[j]) * (blocks >> (j + 1))
        return total

    def copies_of(k, stage):
        if stage < halvings:
            axis, b = order_of(k)[stage]
            size = blocks >> (stage + 1)
            source = start_of(k, stage) + (1 - my_bit(axis, b)) * size
            todo = [(source, size, size, stage, partner(axis, b))]
        else:
            base = start_of(k, halvings)
            todo = []
            for mask in range(1, group):
                device, place = flipped(mask)
                todo.append((base + place, 1, mask, halvings + mask - 1, device))
        return [
            pltpu.make_async_remote_copy(
                src_ref=part.at[k, pl.ds(source, size)],
                dst_ref=recv.at[k, pl.ds(target, size)],
                send_sem=send_sem.at[k, sem],
                recv_sem=recv_sem.at[k, sem],
                device_id=device,
                device_id_type=MESH,
            )
            for source, size, target, sem, device in todo
        ]

    def compute(k):
        for f in range(frames_n):
            unit = f * chunks + k
            tap, col = (unit * width) // channels, (unit * width) % channels
            row_shift, col_shift = tap // taps_side, tap % taps_side
            lo = (taps_side - 1 - row_shift) * cols
            acc = None
            for g in range(frames):
                term = jnp.dot(
                    cot_ref[col_shift, g, :, lo : lo + pixels],
                    mixed_ref[g, :, col : col + width],
                    preferred_element_type=F32,
                )
                acc = term if acc is None else acc + term
            acc = acc.astype(BF16)
            for t in range(tiles_n):
                at = {"tile": t, "frame": f}
                place = 0
                for j, (axis, b) in enumerate(order_of(k)):
                    place += ((at[axis] >> b) & 1) * (blocks >> (j + 1))
                for j, (axis, b) in enumerate(rest):
                    place += ((at[axis] >> b) & 1) << j
                part[k, place] = acc[t * block_rows : (t + 1) * block_rows]

    def merge(k, stage):
        for copy in copies_of(k, stage):
            copy.wait_recv()
        if stage < halvings:
            size = blocks >> (stage + 1)
            mine = start_of(k, stage + 1)
            got = recv[k, size : 2 * size].astype(F32)
            total = part[k, pl.ds(mine, size)].astype(F32) + got
            part[k, pl.ds(mine, size)] = total.astype(BF16)
            for copy in copies_of(k, stage + 1):
                copy.start()
        else:
            total = part[k, start_of(k, halvings) + flipped(0)[1]].astype(F32)
            for mask in range(1, group):
                total = total + recv[k, mask].astype(F32)
            out_ref[:, k * width : (k + 1) * width] = total

    def run():
        due = [2, 5] + [7 + 2 * j for j in range(halvings - 2)] + [7 + 2 * (halvings - 2)]
        for step in range(chunks + due[halvings]):
            for stage in range(halvings, -1, -1):
                k = step - due[stage]
                if 0 <= k < chunks:
                    merge(k, stage)
            if step < chunks:
                compute(step)
                for copy in copies_of(step, 0):
                    copy.start()
        for k in range(chunks):
            for stage in range(halvings + 1):
                for copy in copies_of(k, stage):
                    copy.wait_send()

    return SimpleNamespace(friends=friends, run=run)


def block_kernel(
    lat_hbm, conv_hbm, bias_ref, wq_hbm, wk_hbm, wv_hbm, wo_hbm, cot_hbm,
    mixed_hbm, grad_ref,
    lat_ref, conv_ref, wq, wk, wv, wo, cot_ref, mixed_ref, turned_ref,
    lat_rim, cot_rim, moved, hidden, others, part, recv,
    load_sem, rim_send, rim_recv, hid_send, hid_recv, send_sem, recv_sem,
):
    frames, rows, cols, channels = lat_hbm.shape
    side = conv_hbm.shape[0]
    count, tiles = lax.axis_size("frame"), lax.axis_size("tile")
    frame, tile = lax.axis_index("frame"), lax.axis_index("tile")
    has = (tile > 0, tile < tiles - 1)
    beside = (tile - 1, tile + 1)

    pairs = [
        (lat_hbm, lat_ref), (conv_hbm, conv_ref), (cot_hbm, cot_ref),
        (wq_hbm, wq), (wk_hbm, wk), (wv_hbm, wv), (wo_hbm, wo),
    ]
    loads = [
        pltpu.make_async_copy(source, target, load_sem.at[j])
        for j, (source, target) in enumerate(pairs)
    ]
    for load in loads:
        load.start()
    reduction = reduction_of(side, cols, turned_ref, mixed_ref, grad_ref, part, recv, send_sem, recv_sem)

    barrier = pltpu.get_barrier_semaphore()
    greeted = [{"tile": lax.rem(tile + step, tiles)} for step in (1, tiles - 1)]
    greeted += [{"frame": lax.rem(frame + k, count)} for k in range(1, count)]
    greeted += reduction.friends
    for friend in greeted:
        pl.semaphore_signal(barrier, inc=1, device_id=friend, device_id_type=MESH)
    pl.semaphore_wait(barrier, len(greeted))

    def rim_copy(which, end):
        source, target = ((lat_hbm, lat_rim), (cot_hbm, cot_rim))[which]
        return pltpu.make_async_remote_copy(
            src_ref=source.at[:, (rows - 1) * end],
            dst_ref=target.at[1 - end],
            send_sem=rim_send.at[which, end],
            recv_sem=rim_recv.at[which, 1 - end],
            device_id={"tile": beside[end]},
            device_id_type=MESH,
        )

    def rim_arrival(which, end):
        source, target = ((lat_hbm, lat_rim), (cot_hbm, cot_rim))[which]
        return pltpu.make_async_remote_copy(
            src_ref=source.at[:, (rows - 1) * end],
            dst_ref=target.at[end],
            send_sem=rim_send.at[which, end],
            recv_sem=rim_recv.at[which, end],
            device_id={"tile": beside[end]},
            device_id_type=MESH,
        )

    for which in range(2):
        for end in range(2):

            @pl.when(has[end])
            def _():
                rim_copy(which, end).start()

    def settle(which):
        target = (lat_rim, cot_rim)[which]
        for end in range(2):

            @pl.when(has[end])
            def _():
                rim_arrival(which, end).wait_recv()

            @pl.when(jnp.logical_not(has[end]))
            def _():
                target[end] = jnp.zeros_like(target[end])

    def by_column(value, offset):
        if offset == 0:
            return value
        wide = value.astype(F32)
        rolled = pltpu.roll(wide, (-offset) % cols, 0)
        at = lax.broadcasted_iota(jnp.int32, wide.shape, 0)
        edge = 0 if offset < 0 else cols - 1
        return jnp.where(at == edge, 0.0, rolled).astype(BF16)

    def place(value, f, row):
        for s in range(side):
            moved[s, f, row] = by_column(value, s - 1)

    def convolve(row):
        acc = jnp.broadcast_to(bias_ref[...], (frames * cols, channels))
        for r in range(side):
            for s in range(side):
                acc = acc + jnp.dot(
                    moved[s, :, row + r].reshape(frames * cols, channels),
                    conv_ref[r, s],
                    preferred_element_type=F32,
                )
        result = acc / (1.0 + jnp.exp(-acc))
        hidden[row] = result.astype(BF16)
        for k in range(1, count):
            hidden_copy(k, row).start()

    def hidden_copy(k, row):
        return pltpu.make_async_remote_copy(
            src_ref=hidden.at[row],
            dst_ref=others.at[k - 1, row],
            send_sem=hid_send.at[k - 1, row],
            recv_sem=hid_recv.at[k - 1, row],
            device_id={"frame": lax.rem(frame + k, count)},
            device_id_type=MESH,
        )

    loads[0].wait()
    for row in range(rows):
        for f in range(frames):
            place(lat_ref[f, row], f, row + 1)
    loads[1].wait()
    for row in range(1, rows - 1):
        convolve(row)
    settle(0)
    for f in range(frames):
        place(lat_rim[0, f], f, 0)
        place(lat_rim[1, f], f, rows + 1)
    for row in (rows - 1, 0):
        convolve(row)

    def turn(value, f, row):
        for s in range(side):
            turned_ref[s, f, :, row * cols : (row + 1) * cols] = by_column(value, 1 - s).T

    loads[2].wait()
    for row in range(rows):
        for f in range(frames):
            turn(cot_ref[f, row], f, row + 1)
    settle(1)
    for f in range(frames):
        turn(cot_rim[0, f], f, 0)
        turn(cot_rim[1, f], f, rows + 1)

    for load in loads[3:]:
        load.wait()

    def attend_row(i, carry):
        row = lax.rem(i + 1, rows)
        for k in range(1, count):
            hidden_copy(k, row).wait_recv()
        parts = [hidden[row]] + [others[k - 1, row] for k in range(1, count)]
        mixed = attend(parts, wq, wk, wv, wo, frames)
        for f in range(frames):
            mixed_ref[f, pl.ds(pl.multiple_of(row * cols, cols), cols)] = mixed[
                f * cols : (f + 1) * cols
            ]
        return carry

    lax.fori_loop(0, rows, attend_row, 0)
    store = pltpu.make_async_copy(mixed_ref, mixed_hbm, load_sem.at[0])
    store.start()
    reduction.run()
    store.wait()
    for row in range(rows):
        for k in range(1, count):
            hidden_copy(k, row).wait_send()
    for which in range(2):
        for end in range(2):

            @pl.when(has[end])
            def _():
                rim_copy(which, end).wait_send()


def block(latents, conv_weight, conv_bias, wq, wk, wv, wo, cotangent):
    frames, rows, cols, channels = latents.shape
    side = conv_weight.shape[0]
    out_channels = cotangent.shape[3]
    count, tiles_n = lax.axis_size("frame"), lax.axis_size("tile")
    chunks, width = side * side, channels // count
    blocks, block_rows = count * tiles_n, out_channels // tiles_n
    orders, rest = split_bits(count, tiles_n)
    stages = len(orders[0]) + (1 << len(rest)) - 1
    hbm = pl.BlockSpec(memory_space=pltpu.HBM)
    vmem = pl.BlockSpec(memory_space=pltpu.VMEM)
    square = pltpu.VMEM((channels, channels), BF16)
    return pl.pallas_call(
        block_kernel,
        out_shape=[
            jax.ShapeDtypeStruct((frames, rows * cols, channels), BF16),
            jax.ShapeDtypeStruct((block_rows, chunks * width), F32),
        ],
        in_specs=[hbm, hbm, vmem] + [hbm] * 5,
        out_specs=[hbm, vmem],
        scratch_shapes=[
            pltpu.VMEM(latents.shape, BF16),
            pltpu.VMEM(conv_weight.shape, BF16),
            square, square, square, square,
            pltpu.VMEM(cotangent.shape, BF16),
            pltpu.VMEM((frames, rows * cols, channels), BF16),
            pltpu.VMEM((side, frames, out_channels, (rows + 2) * cols), BF16),
            pltpu.VMEM((2, frames, cols, channels), BF16),
            pltpu.VMEM((2, frames, cols, channels), BF16),
            pltpu.VMEM((side, frames, rows + 2, cols, channels), BF16),
            pltpu.VMEM((rows, frames * cols, channels), BF16),
            pltpu.VMEM((count - 1, rows, frames * cols, channels), BF16),
            pltpu.VMEM((chunks, blocks, block_rows, width), BF16),
            pltpu.VMEM((chunks, blocks, block_rows, width), BF16),
            pltpu.SemaphoreType.DMA((7,)),
            pltpu.SemaphoreType.DMA((2, 2)),
            pltpu.SemaphoreType.DMA((2, 2)),
            pltpu.SemaphoreType.DMA((count - 1, rows)),
            pltpu.SemaphoreType.DMA((count - 1, rows)),
            pltpu.SemaphoreType.DMA((chunks, stages)),
            pltpu.SemaphoreType.DMA((chunks, stages)),
        ],
        compiler_params=pltpu.CompilerParams(
            collective_id=0, has_side_effects=True, vmem_limit_bytes=63 * 1024 * 1024
        ),
    )(latents, conv_weight, conv_bias.reshape(1, -1), wq, wk, wv, wo, cotangent)


def on_device(
    latents, conv_weight, conv_bias, query_weight, key_weight, value_weight, out_weight, cotangent
):
    frames, rows, cols, channels = latents.shape
    mixed, conv_grad = block(
        latents, conv_weight, conv_bias, query_weight, key_weight, value_weight, out_weight, cotangent
    )
    return (mixed.reshape(frames, rows, cols, channels), conv_grad)


def solution(mesh):
    in_specs = (
        P("frame", "tile", None, None),
        P(),
        P(),
        P(),
        P(),
        P(),
        P(),
        P("frame", "tile", None, None),
    )
    out_specs = (P("frame", "tile", None, None), P("tile", "frame"))
    return jax.shard_map(
        on_device, mesh=mesh, in_specs=in_specs, out_specs=out_specs, check_vma=False
    )
```
